32 devices in a mesh: dp: 2 (over x), seq: 16 (over z, y, core).
Axes of the slice: x: 2, y: 2, z: 4, core: 2. Of those that a mesh axis runs over, the one named last changes fastest.
Arguments:
- layer_input: bfloat16 [2, 2048, 768], P('dp', 'seq'), may hold values from -6 to 6
- ln1_gain: bfloat16 [768], P(('dp', 'seq')), may hold values from 0.5 to 1.5
- ln1_bias: bfloat16 [768], P(('dp', 'seq')), may hold values from -3 to 3
- w_qkv: bfloat16 [768, 2304], P(('dp', 'seq')), may hold values from -0.21875 to 0.21875
- bias_query: bfloat16 [768], P(('dp', 'seq')), may hold values from -3 to 3
- bias_value: bfloat16 [768], P(('dp', 'seq')), may hold values from -3 to 3
- w_attn_out: bfloat16 [768, 768], P(('dp', 'seq')), may hold values from -1.25 to 1.25
- bias_attn_out: bfloat16 [768], P(('dp', 'seq')), may hold values from -3 to 3
- ln2_gain: bfloat16 [768], P(('dp', 'seq')), may hold values from 0.5 to 1.5
- ln2_bias: bfloat16 [768], P(('dp', 'seq')), may hold values from -3 to 3
- w_fc: bfloat16 [768, 3072], P(('dp', 'seq')), may hold values from -0.21875 to 0.21875
- bias_fc: bfloat16 [3072], P(('dp', 'seq')), may hold values from -3 to 3
- w_proj: bfloat16 [3072, 768], P(('dp', 'seq')), may hold values from -0.109375 to 0.109375
- bias_proj: bfloat16 [768], P(('dp', 'seq')), may hold values from -3 to 3
- segment_ids: int32 [2, 2048], P('dp', 'seq'), may hold values from 0 to 3, never falling along the last dimension, each value on 1 to 1280 neighbouring positions
- cotangent: bfloat16 [2, 2048, 768], P('dp', 'seq'), may hold values from -6 to 6
Outputs:
- layer_output: bfloat16 [2, 2048, 768], P('dp', 'seq')
- grad_input: bfloat16 [2, 2048, 768], P('dp', 'seq')
- grad_ln1_gain: float32 [768], P(('dp', 'seq'))
- grad_ln1_bias: float32 [768], P(('dp', 'seq'))
- grad_w_qkv: float32 [768, 2304], P(('dp', 'seq'))
- grad_bias_query: float32 [768], P(('dp', 'seq'))
- grad_bias_value: float32 [768], P(('dp', 'seq'))
- grad_w_attn_out: float32 [768, 768], P(('dp', 'seq'))
- grad_bias_attn_out: float32 [768], P(('dp', 'seq'))
- grad_ln2_gain: float32 [768], P(('dp', 'seq'))
- grad_ln2_bias: float32 [768], P(('dp', 'seq'))
- grad_w_fc: float32 [768, 3072], P(('dp', 'seq'))
- grad_bias_fc: float32 [3072], P(('dp', 'seq'))
- grad_w_proj: float32 [3072, 768], P(('dp', 'seq'))
- grad_bias_proj: float32 [768], P(('dp', 'seq'))
The draws below stay inside these ranges and needn't reach their ends.
Inputs may be any that keep to these rules, and one draw needn't show every extreme that they name: `segment_ids`: in each sequence the ids start at 0, never fall, and each of the 4 ids covers 1 to 1280 consecutive positions, one of them exactly 1280.
All inputs are finite; a program needn't handle non-finite values.
Results may differ from the reference program's by a relative error of at most 0.012.
The reference program's roundings to bfloat16 on the way count: a program that leaves them out, or rounds other values in their place, can miss the bound.
Values may be sent and summed in bfloat16 or wider, within the bound.
No kernel may reach another device: no remote copies, remote signals or barrier semaphores. Data moves between devices by JAX's collectives and lax.ppermute only.
A program may use at most 192 MiB of HBM per device.

```python
import math
import jax
import jax.numpy as jnp
import numpy as np
from jax import lax

D = 768
HEADS = 12
HEAD_DIM = 64
FF = 3072
TOK_DEV = 128
DOCS = 4
LENGTH = 2048
SEQS = 2


def raised(drawn, stream_key, source, target, parts, factor):
    def block_of(dim):
        return (jnp.arange(drawn.shape[dim]) // (drawn.shape[dim] // parts)).reshape((-1,) + (1,) * (drawn.ndim - 1 - dim))

    first = jax.random.permutation(stream_key, parts)[block_of(target)]
    far = (block_of(target) + parts // 2) % parts
    return jnp.where((block_of(source) == first) | (block_of(source) == far), factor * drawn, drawn)


def block_levels(stream_key, extent, cuts, low, largest):
    factor_of, own = 1.0, jax.random.fold_in(stream_key, 6)
    for position, blocks in cuts:
        draws = jnp.exp(jax.random.uniform(jax.random.fold_in(own, position), (blocks,), jnp.float32, low / len(cuts), largest / len(cuts)))
        factor_of = factor_of * jnp.repeat(draws, extent[position] // blocks).reshape([-1 if axis == position else 1 for axis in range(len(extent))])
    return factor_of


def split_up(number_of, total, limit, skew):
    loads = [(1 << 20) // math.isqrt(rank ** skew) + 1 for rank in range(2, number_of + 1)]
    rest, holding = total - limit - (number_of - 1), [1] * (number_of - 1)
    while rest > 0:
        free = [i for i in range(number_of - 1) if holding[i] < limit]
        mass, budget = sum([loads[i] for i in free]), rest
        for i in free:
            extra = min(limit - holding[i], max(1, budget * loads[i] // mass), rest)
            holding[i] = holding[i] + extra
            rest = rest - extra
    return np.array([limit] + holding)


def uneven(own_key, amount, total, bound, skew):
    if amount == 2:
        one = jax.random.randint(own_key, (), max(1, total - bound), min(bound, total - 1) + 1)
        return jnp.stack([one, total - one])
    sizes = jnp.asarray(split_up(amount, total, bound, skew), jnp.int32)
    couples = (amount - 1) // 2
    giver, taker = sizes[1:1 + 2 * couples:2], sizes[2:2 + 2 * couples:2]
    margin = jnp.minimum(giver - 1, bound - taker)
    moved = jax.random.randint(jax.random.fold_in(own_key, 1), (couples,), 0, 1 << 20) % (margin + 1)
    sizes = sizes.at[1:1 + 2 * couples:2].set(giver - moved).at[2:2 + 2 * couples:2].set(taker + moved)
    return sizes[jax.random.permutation(jax.random.fold_in(own_key, 2), amount)]


def noise(key, dims, scale, bound, cuts=(), kind=jnp.bfloat16):
    level = block_levels(key, dims, cuts, -0.22, 0.18) if cuts else 1.0
    entries = jax.random.normal(key, dims, jnp.float32) * scale * level
    return jnp.minimum(jnp.maximum(entries, -bound), bound).astype(kind)


def bell_draw_with(key, dims, spread, most, pieces, heavy, held_as=jnp.bfloat16):
    drawn = spread * jax.random.normal(key, dims, jnp.float32)
    if pieces:
        drawn = drawn * block_levels(key, dims, pieces, -0.22, 0.18)
    return jnp.clip(raised(drawn, jax.random.fold_in(key, 3), *heavy), -most, most).astype(held_as)


def setup_inputs(seed: int = 0) -> dict:
    seeds = jax.random.split(jax.random.key(seed), 17)
    layer_input = noise(seeds[0], (SEQS, LENGTH, D), 1.0, 6.0, ((0, 2), (1, 16)))
    ln1_gain = jnp.clip(1.0 + 0.1 * jax.random.normal(seeds[1], (D,), jnp.float32), 0.5, 1.5).astype(jnp.bfloat16)
    ln1_bias = noise(seeds[2], (D,), 0.5, 3.0, ((0, 32),))
    w_qkv = noise(seeds[3], (D, 3 * D), D ** -0.5, 0.21875, ((0, 32),))
    bias_query = noise(seeds[4], (D,), 0.5, 3.0, ((0, 32),))
    bias_value = noise(seeds[5], (D,), 0.5, 3.0, ((0, 32),))
    w_attn_out = noise(seeds[6], (D, D), (D // 32) ** -0.5, 1.25, ((0, 32),))
    bias_attn_out = noise(seeds[7], (D,), 0.5, 3.0, ((0, 32),))
    ln2_gain = jnp.clip(1.0 + 0.1 * jax.random.normal(seeds[8], (D,), jnp.float32), 0.5, 1.5).astype(jnp.bfloat16)
    ln2_bias = noise(seeds[9], (D,), 0.5, 3.0, ((0, 32),))
    w_fc = noise(seeds[10], (D, FF), D ** -0.5, 0.21875, ((0, 32),))
    bias_fc = noise(seeds[11], (FF,), 0.5, 3.0, ((0, 32),))
    w_proj = noise(seeds[12], (FF, D), FF ** -0.5, 0.109375, ((0, 32),))
    bias_proj = noise(seeds[13], (D,), 0.5, 3.0, ((0, 32),))
    segment_ids = jax.vmap(lambda own: jnp.searchsorted(jnp.cumsum(uneven(own, DOCS, LENGTH, LENGTH // 2 + 2 * TOK_DEV, 0)), jnp.arange(LENGTH), side="right"))(jax.random.split(seeds[14], SEQS)).reshape((SEQS, LENGTH)).astype(jnp.int32)
    cotangent = bell_draw_with(seeds[15], (SEQS, LENGTH, D), 1.0, 6.0, ((0, 2), (1, 16)), (1, 2, 16, 2.0))
    return dict(layer_input=layer_input, ln1_gain=ln1_gain, ln1_bias=ln1_bias, w_qkv=w_qkv, bias_query=bias_query, bias_value=bias_value, w_attn_out=w_attn_out, bias_attn_out=bias_attn_out, ln2_gain=ln2_gain, ln2_bias=ln2_bias, w_fc=w_fc, bias_fc=bias_fc, w_proj=w_proj, bias_proj=bias_proj, segment_ids=segment_ids, cotangent=cotangent)


EPS = 1e-05
SCALE = 0.125
NEG = -1e+30
GELU_C = math.sqrt(2.0 / math.pi)

def norm_fwd(x_float, gain, bias):
    mean_val = lax.optimization_barrier(jnp.mean(x_float, -1, keepdims=True))
    centred = x_float - mean_val
    inv_std = lax.rsqrt(lax.optimization_barrier(jnp.mean(centred * centred, -1, keepdims=True)) + EPS)
    normed = centred * inv_std
    return (normed, inv_std, normed * gain.astype(jnp.float32) + bias.astype(jnp.float32))

def norm_back(d_norm, normed, inv_std, gain):
    scaled = d_norm * gain.astype(jnp.float32)
    d_in = inv_std * (scaled - lax.optimization_barrier(jnp.mean(scaled, -1, keepdims=True)) - normed * lax.optimization_barrier(jnp.mean(scaled * normed, -1, keepdims=True)))
    return (d_in, lax.optimization_barrier(jnp.sum(d_norm * normed, 0)), lax.optimization_barrier(jnp.sum(d_norm, 0)))

def gelu_pair(pre_act):
    inner = GELU_C * (pre_act + 0.044715 * pre_act * pre_act * pre_act)
    tanh_val = jnp.tanh(inner)
    value = 0.5 * pre_act * (1.0 + tanh_val)
    slope = 0.5 * (1.0 + tanh_val) + 0.5 * pre_act * (1.0 - tanh_val * tanh_val) * GELU_C * (1.0 + 3.0 * 0.044715 * pre_act * pre_act)
    return (value, slope)

def layer(x_seq, seg_seq, dy_seq, params):
    ln1_gain, ln1_bias, w_qkv, bias_query, bias_value, w_attn_out, bias_attn_out, ln2_gain, ln2_bias, w_fc, bias_fc, w_proj, bias_proj = params
    length = x_seq.shape[0]
    width = x_seq.shape[1]
    block = math.gcd(length, 512)
    count = length // block
    positions = jnp.arange(length, dtype=jnp.int32)
    x_float = x_seq.astype(jnp.float32)
    normed1, inv1, pre1 = norm_fwd(x_float, ln1_gain, ln1_bias)
    n1 = pre1.astype(jnp.bfloat16)
    qkv = jnp.dot(n1, w_qkv, preferred_element_type=jnp.float32)
    queries = (qkv[:, :width] + bias_query.astype(jnp.float32)).astype(jnp.bfloat16)
    keys_all = qkv[:, width:2 * width].astype(jnp.bfloat16)
    values_all = (qkv[:, 2 * width:] + bias_value.astype(jnp.float32)).astype(jnp.bfloat16)
    keys_h = keys_all.reshape(length, HEADS, HEAD_DIM).astype(jnp.float32)
    values_h = values_all.reshape(length, HEADS, HEAD_DIM).astype(jnp.float32)
    q_blocks = queries.reshape(count, block, HEADS, HEAD_DIM)
    pos_blocks = positions.reshape(count, block)
    seg_blocks = seg_seq.reshape(count, block)

    def scores_of(q_blk, pos_blk, seg_blk):
        scores = jnp.einsum('qhd,khd->qhk', q_blk.astype(jnp.float32), keys_h) * SCALE
        visible = ((positions[None, :] <= pos_blk[:, None]) & (seg_seq[None, :] == seg_blk[:, None]))[:, None, :]
        return (jnp.where(visible, scores, NEG), visible)

    def attend(args):
        q_blk, pos_blk, seg_blk = args
        scores, visible = scores_of(q_blk, pos_blk, seg_blk)
        top = lax.optimization_barrier(jnp.max(scores, -1))
        total = lax.optimization_barrier(jnp.sum(jnp.where(visible, jnp.exp(scores - top[..., None]), 0.0), -1))
        lse = top + jnp.log(total)
        probs = jnp.where(visible, jnp.exp(scores - lse[..., None]), 0.0)
        out = jnp.einsum('qhk,khd->qhd', probs, values_h, precision=lax.Precision.HIGHEST)
        return (out, lse)
    attn_f, lse_all = lax.map(attend, (q_blocks, pos_blocks, seg_blocks))
    attn = attn_f.reshape(length, width).astype(jnp.bfloat16)
    hid = x_float + jnp.dot(attn, w_attn_out, preferred_element_type=jnp.float32) + bias_attn_out.astype(jnp.float32)
    normed2, inv2, pre2 = norm_fwd(hid, ln2_gain, ln2_bias)
    n2 = pre2.astype(jnp.bfloat16)
    pre_act = jnp.dot(n2, w_fc, preferred_element_type=jnp.float32) + bias_fc.astype(jnp.float32)
    act_f, slope = gelu_pair(pre_act)
    act = act_f.astype(jnp.bfloat16)
    out = (hid + jnp.dot(act, w_proj, preferred_element_type=jnp.float32) + bias_proj.astype(jnp.float32)).astype(jnp.bfloat16)
    dy_float = dy_seq.astype(jnp.float32)
    g_w_proj = jnp.dot(act.T, dy_seq, preferred_element_type=jnp.float32)
    g_bias_proj = lax.optimization_barrier(jnp.sum(dy_float, 0))
    d_pre_f = jnp.dot(dy_seq, w_proj.T, preferred_element_type=jnp.float32) * slope
    d_pre = d_pre_f.astype(jnp.bfloat16)
    g_w_fc = jnp.dot(n2.T, d_pre, preferred_element_type=jnp.float32)
    g_bias_fc = lax.optimization_barrier(jnp.sum(d_pre_f, 0))
    d_n2 = jnp.dot(d_pre, w_fc.T, preferred_element_type=jnp.float32)
    d_from2, g_ln2_gain, g_ln2_bias = norm_back(d_n2, normed2, inv2, ln2_gain)
    d_hid_f = dy_float + d_from2
    d_hid = d_hid_f.astype(jnp.bfloat16)
    g_w_attn_out = jnp.dot(attn.T, d_hid, preferred_element_type=jnp.float32)
    g_bias_attn_out = lax.optimization_barrier(jnp.sum(d_hid_f, 0))
    d_attn = jnp.dot(d_hid, w_attn_out.T, preferred_element_type=jnp.float32).astype(jnp.bfloat16)
    d_attn_h = d_attn.reshape(length, HEADS, HEAD_DIM).astype(jnp.float32)
    delta = lax.optimization_barrier(jnp.sum(d_attn_h * attn.reshape(length, HEADS, HEAD_DIM).astype(jnp.float32), -1))
    d_blocks = d_attn_h.reshape(count, block, HEADS, HEAD_DIM)
    delta_blocks = delta.reshape(count, block, HEADS)

    def back_step(carry, args):
        d_keys, d_values = carry
        q_blk, pos_blk, seg_blk, lse, d_out, dl = args
        scores, visible = scores_of(q_blk, pos_blk, seg_blk)
        probs = jnp.where(visible, jnp.exp(scores - lse[..., None]), 0.0)
        d_prob = jnp.einsum('qhd,khd->qhk', d_out, values_h)
        d_score = (probs * (d_prob - dl[..., None])).astype(jnp.bfloat16).astype(jnp.float32)
        probs_b = probs.astype(jnp.bfloat16).astype(jnp.float32)
        d_q = jnp.einsum('qhk,khd->qhd', d_score, keys_h) * SCALE
        d_keys = d_keys + jnp.einsum('qhk,qhd->khd', d_score, q_blk.astype(jnp.float32)) * SCALE
        d_values = d_values + jnp.einsum('qhk,qhd->khd', probs_b, d_out)
        return ((d_keys, d_values), d_q)
    zero_h = jnp.zeros((length, HEADS, HEAD_DIM), jnp.float32)
    (d_keys, d_values), d_q_blocks = lax.scan(back_step, (zero_h, zero_h), (q_blocks, pos_blocks, seg_blocks, lse_all, d_blocks, delta_blocks))
    d_queries = d_q_blocks.reshape(length, width)
    d_keys = d_keys.reshape(length, width)
    d_values = d_values.reshape(length, width)
    g_bias_query = lax.optimization_barrier(jnp.sum(d_queries, 0))
    g_bias_value = lax.optimization_barrier(jnp.sum(d_values, 0))
    d_qkv = jnp.concatenate([d_queries, d_keys, d_values], -1).astype(jnp.bfloat16)
    g_w_qkv = jnp.dot(n1.T, d_qkv, preferred_element_type=jnp.float32)
    d_n1 = jnp.dot(d_qkv, w_qkv.T, preferred_element_type=jnp.float32)
    d_from1, g_ln1_gain, g_ln1_bias = norm_back(d_n1, normed1, inv1, ln1_gain)
    grad_in = (d_hid_f + d_from1).astype(jnp.bfloat16)
    grads = (g_ln1_gain, g_ln1_bias, g_w_qkv, g_bias_query, g_bias_value, g_w_attn_out, g_bias_attn_out, g_ln2_gain, g_ln2_bias, g_w_fc, g_bias_fc, g_w_proj, g_bias_proj)
    return (out, grad_in, grads)

def reference(layer_input, ln1_gain, ln1_bias, w_qkv, bias_query, bias_value, w_attn_out, bias_attn_out, ln2_gain, ln2_bias, w_fc, bias_fc, w_proj, bias_proj, segment_ids, cotangent):
    params = (ln1_gain, ln1_bias, w_qkv, bias_query, bias_value, w_attn_out, bias_attn_out, ln2_gain, ln2_bias, w_fc, bias_fc, w_proj, bias_proj)
    zeros = tuple((jnp.zeros(weight.shape, jnp.float32) for weight in params))

    def one_seq(sums, inputs):
        x_seq, seg_seq, dy_seq = inputs
        out, grad_in, grads = layer(x_seq, seg_seq, dy_seq, params)
        return (tuple((left + right for left, right in zip(sums, grads))), (out, grad_in))
    sums, (outputs, grad_input) = lax.scan(one_seq, zeros, (layer_input, segment_ids, cotangent))
    return (outputs, grad_input, sums[0], sums[1], sums[2], sums[3], sums[4], sums[5], sums[6], sums[7], sums[8], sums[9], sums[10], sums[11], sums[12])
```

```python
import functools
import math

import jax
import jax.numpy as jnp
from jax import lax
from jax.experimental import pallas as pl
from jax.experimental.pallas import tpu as pltpu
from jax.sharding import PartitionSpec as P

HEADS = 12
EPS = 1e-05
SCALE = 0.125
NEG = -1e30
GELU_C = math.sqrt(2.0 / math.pi)
BF = jnp.bfloat16
F32 = jnp.float32
LANES = 128
NN = (((1,), (0,)), ((), ()))
NT = (((1,), (1,)), ((), ()))
TN = (((0,), (0,)), ((), ()))


def mm(a, b, dims=NN):
    return lax.dot_general(a, b, dims, preferred_element_type=F32)


def norm_fwd(x_float, gain, bias):
    mean_val = jnp.mean(x_float, -1, keepdims=True)
    centred = x_float - mean_val
    inv_std = lax.rsqrt(jnp.mean(centred * centred, -1, keepdims=True) + EPS)
    normed = centred * inv_std
    return (normed, inv_std, normed * gain + bias)


def norm_back(d_norm, normed, inv_std, gain):
    scaled = d_norm * gain
    d_in = inv_std * (
        scaled
        - jnp.mean(scaled, -1, keepdims=True)
        - normed * jnp.mean(scaled * normed, -1, keepdims=True)
    )
    return (d_in, jnp.sum(d_norm * normed, 0), jnp.sum(d_norm, 0))


def gelu_pair(pre_act):
    inner = GELU_C * (pre_act + 0.044715 * pre_act * pre_act * pre_act)
    tanh_val = jnp.tanh(inner)
    value = 0.5 * pre_act * (1.0 + tanh_val)
    slope = 0.5 * (1.0 + tanh_val) + 0.5 * pre_act * (1.0 - tanh_val * tanh_val) * GELU_C * (
        1.0 + 3.0 * 0.044715 * pre_act * pre_act
    )
    return (value, slope)


class Grid:
    def __init__(self, mesh):
        seq = mesh.shape["seq"]
        core = 2
        chips = seq // core
        z = math.gcd(chips, 4)
        self.sizes = {"d": mesh.shape["dp"], "z": z, "y": chips // z, "c": core}
        self.order = ("d", "z", "y", "c")

    def size(self, dim):
        return self.sizes[dim]

    def index(self, dim):
        if dim == "d":
            return lax.axis_index("dp")
        rest = lax.axis_index("seq")
        for name in ("c", "y", "z"):
            if name == dim:
                return rest % self.sizes[name]
            rest = rest // self.sizes[name]

    def shift(self, value, dim, step):
        total = math.prod(self.sizes.values())
        stride = 1
        for name in reversed(self.order):
            if name == dim:
                break
            stride *= self.sizes[name]
        n = self.sizes[dim]
        pairs = []
        for dev in range(total):
            at = dev // stride % n
            pairs.append((dev, dev + ((at + step) % n - at) * stride))
        return lax.ppermute(value, ("dp", "seq"), pairs)

    def gather(self, value, dim, axis=0):
        n = self.sizes[dim]
        if n == 1:
            return jnp.expand_dims(value, axis)
        at = self.index(dim)
        if n == 2:
            return pair(value, self.shift(value, dim, 1), at, axis)
        got = [value] + [self.shift(value, dim, k) for k in range(1, n)]
        shape = value.shape[:axis] + (n,) + value.shape[axis:]
        buf = jnp.zeros(shape, value.dtype)
        for k, blk in enumerate(got):
            buf = lax.dynamic_update_slice_in_dim(
                buf, jnp.expand_dims(blk, axis), (at - k) % n, axis
            )
        return buf

    def scatter(self, value, dim, axis=0, wire=BF):
        n = self.sizes[dim]
        if n == 1:
            return lax.squeeze(value, (axis,)).astype(F32)
        at = self.index(dim)
        pick = lambda k: lax.dynamic_index_in_dim(value, (at + k) % n, axis, keepdims=False)
        got = [self.shift(pick(k).astype(wire), dim, k) for k in range(1, n)]
        total = pick(0).astype(F32)
        for blk in got:
            total = total + blk.astype(F32)
        return total


def pair(own, other, at, axis=0):
    first = at == 0
    return jnp.stack([jnp.where(first, own, other), jnp.where(first, other, own)], axis)


def attn_fwd_kernel(bounds, q_ref, k_ref, v_ref, pos_ref, out_ref, lse_ref, s_ref, *, blk):
    lo, hi = bounds[0], bounds[1]
    rows = q_ref.shape[0]
    q = q_ref[...].astype(F32)
    lane = lax.broadcasted_iota(jnp.int32, q.shape, 1)
    q_pos = pos_ref[0:1, :]
    q_start = pos_ref[1:2, :]
    base = lax.broadcasted_iota(jnp.int32, (blk, rows), 0)
    outs = []
    for h in range(2):
        mine = (lane < 64) if h == 0 else (lane >= 64)
        qh = jnp.where(mine, q, 0.0).astype(BF)

        def scan_max(i, top):
            off = pl.multiple_of(i * blk, blk)
            s = mm(k_ref[pl.ds(off, blk), :], qh, NT) * SCALE
            k_pos = base + off
            s = jnp.where((k_pos <= q_pos) & (k_pos >= q_start), s, NEG)
            s_ref[pl.ds(off, blk), :] = s
            return jnp.maximum(top, jnp.max(s, axis=0, keepdims=True))

        top = lax.fori_loop(lo, hi, scan_max, jnp.full((1, rows), NEG, F32))

        def scan_sum(i, carry):
            total, acc = carry
            off = pl.multiple_of(i * blk, blk)
            p = jnp.exp(s_ref[pl.ds(off, blk), :] - top)
            total = total + jnp.sum(p, axis=0, keepdims=True)
            p_hi = p.astype(BF)
            p_lo = (p - p_hi.astype(F32)).astype(BF)
            vb = v_ref[pl.ds(off, blk), :]
            return (total, acc + mm(vb, p_hi, TN) + mm(vb, p_lo, TN))

        total, acc = lax.fori_loop(
            lo, hi, scan_sum, (jnp.zeros((1, rows), F32), jnp.zeros((LANES, rows), F32))
        )
        lse_ref[0, h : h + 1, :] = top + jnp.log(total)
        outs.append(acc / total)
    sub = lax.broadcasted_iota(jnp.int32, (LANES, rows), 0)
    out_ref[...] = jnp.where(sub < 64, outs[0], outs[1]).T.astype(BF)


def attn_bwd_kernel(
    bounds, q_ref, k_ref, v_ref, do_ref, o_ref, lse_ref, pos_ref, dq_ref, dk_ref, dv_ref, *, blk
):
    lo, hi = bounds[0], bounds[1]
    rows = q_ref.shape[0]
    q = q_ref[...].astype(F32)
    do = do_ref[...].astype(F32)
    lane = lax.broadcasted_iota(jnp.int32, q.shape, 1)
    q_pos = pos_ref[0:1, :]
    q_start = pos_ref[1:2, :]
    base = lax.broadcasted_iota(jnp.int32, (blk, rows), 0)
    prod = (do * o_ref[...].astype(F32)).T
    delta = [jnp.sum(prod[:64], 0, keepdims=True), jnp.sum(prod[64:], 0, keepdims=True)]
    qs = [jnp.where(lane < 64, q, 0.0).astype(BF), jnp.where(lane >= 64, q, 0.0).astype(BF)]
    dos = [jnp.where(lane < 64, do, 0.0).astype(BF), jnp.where(lane >= 64, do, 0.0).astype(BF)]
    lse = [lse_ref[0, 0:1, :], lse_ref[0, 1:2, :]]
    dk_ref[...] = jnp.zeros_like(dk_ref)
    dv_ref[...] = jnp.zeros_like(dv_ref)

    def step(i, carry):
        off = pl.multiple_of(i * blk, blk)
        kb = k_ref[pl.ds(off, blk), :]
        vb = v_ref[pl.ds(off, blk), :]
        k_pos = base + off
        seen = (k_pos <= q_pos) & (k_pos >= q_start)
        dk = jnp.zeros((blk, LANES), F32)
        dv = jnp.zeros((blk, LANES), F32)
        new = []
        for h in range(2):
            s = jnp.where(seen, mm(kb, qs[h], NT) * SCALE, NEG)
            p = jnp.where(seen, jnp.exp(s - lse[h]), 0.0)
            ds = (p * (mm(vb, dos[h], NT) - delta[h])).astype(BF)
            dv = dv + mm(p.astype(BF), dos[h])
            dk = dk + mm(ds, qs[h])
            new.append(carry[h] + mm(kb, ds, TN))
        dk_ref[pl.ds(off, blk), :] = (dk * SCALE).astype(dk_ref.dtype)
        dv_ref[pl.ds(off, blk), :] = dv.astype(dv_ref.dtype)
        return tuple(new)

    zero = jnp.zeros((LANES, rows), F32)
    dqs = lax.fori_loop(lo, hi, step, (zero, zero))
    sub = lax.broadcasted_iota(jnp.int32, (LANES, rows), 0)
    dq_ref[...] = (jnp.where(sub < 64, dqs[0], dqs[1]) * SCALE).T


def attn_fwd(bounds, queries, keys, values, pos):
    rows, width = queries.shape
    length = keys.shape[0]
    pairs = width // LANES
    blk = math.gcd(length, 256)
    col = lambda p, b: (0, p)
    return pl.pallas_call(
        functools.partial(attn_fwd_kernel, blk=blk),
        grid_spec=pltpu.PrefetchScalarGridSpec(
            num_scalar_prefetch=1,
            grid=(pairs,),
            in_specs=[
                pl.BlockSpec((rows, LANES), col),
                pl.BlockSpec((length, LANES), col),
                pl.BlockSpec((length, LANES), col),
                pl.BlockSpec((2, rows), lambda p, b: (0, 0)),
            ],
            out_specs=[
                pl.BlockSpec((rows, LANES), col),
                pl.BlockSpec((1, 2, rows), lambda p, b: (p, 0, 0)),
            ],
            scratch_shapes=[pltpu.VMEM((length, rows), F32)],
        ),
        out_shape=(
            jax.ShapeDtypeStruct((rows, width), BF),
            jax.ShapeDtypeStruct((pairs, 2, rows), F32),
        ),
        name="attn_fwd",
    )(bounds, queries, keys, values, pos)


def attn_bwd(bounds, queries, keys, values, d_attn, attn, lse, pos):
    rows, width = queries.shape
    length = keys.shape[0]
    pairs = width // LANES
    blk = math.gcd(length, 256)
    col = lambda p, b: (0, p)
    return pl.pallas_call(
        functools.partial(attn_bwd_kernel, blk=blk),
        grid_spec=pltpu.PrefetchScalarGridSpec(
            num_scalar_prefetch=1,
            grid=(pairs,),
            in_specs=[
                pl.BlockSpec((rows, LANES), col),
                pl.BlockSpec((length, LANES), col),
                pl.BlockSpec((length, LANES), col),
                pl.BlockSpec((rows, LANES), col),
                pl.BlockSpec((rows, LANES), col),
                pl.BlockSpec((1, 2, rows), lambda p, b: (p, 0, 0)),
                pl.BlockSpec((2, rows), lambda p, b: (0, 0)),
            ],
            out_specs=[
                pl.BlockSpec((rows, LANES), col),
                pl.BlockSpec((length, LANES), col),
                pl.BlockSpec((length, LANES), col),
            ],
        ),
        out_shape=(
            jax.ShapeDtypeStruct((rows, width), F32),
            jax.ShapeDtypeStruct((length, width), BF),
            jax.ShapeDtypeStruct((length, width), BF),
        ),
        name="attn_bwd",
    )(bounds, queries, keys, values, d_attn, attn, lse, pos)


def body(
    grid,
    layer_input,
    ln1_gain,
    ln1_bias,
    w_qkv,
    bias_query,
    bias_value,
    w_attn_out,
    bias_attn_out,
    ln2_gain,
    ln2_bias,
    w_fc,
    bias_fc,
    w_proj,
    bias_proj,
    segment_ids,
    cotangent,
):
    nd, nz, ny, nc = (grid.size(k) for k in ("d", "z", "y", "c"))
    chips = nd * nz * ny
    devs = chips * nc
    per = ln1_gain.shape[0]
    width = per * devs
    half = width // nc
    per_ff = bias_fc.shape[0]
    ff_half = per_ff * chips
    ff_rows = per_ff // per
    tok = layer_input.shape[1]
    core = grid.index("c")
    chip_at = grid.index("z") * ny + grid.index("y")

    seg_rows = -(-tok // per)
    seg_own = jnp.pad(segment_ids[0].astype(BF), (0, seg_rows * per - tok)).reshape(seg_rows, per)
    small = jnp.concatenate(
        [
            jnp.stack(
                [
                    ln1_gain,
                    ln1_bias,
                    bias_query,
                    bias_value,
                    bias_attn_out,
                    ln2_gain,
                    ln2_bias,
                    bias_proj,
                ]
            ),
            bias_fc.reshape(ff_rows, per),
            seg_own,
        ]
    )
    small = grid.gather(small, "c")
    small = grid.gather(small, "z")
    small = grid.gather(small, "y", axis=1)
    seg_all = small[:, :, :, 8 + ff_rows :].reshape(nz * ny * nc, seg_rows * per)[:, :tok]
    seg_all = seg_all.reshape(nz * ny * nc * tok)
    small = grid.gather(small[:, :, :, : 8 + ff_rows], "d").reshape(devs, 8 + ff_rows, per)
    params = small[:, :8].transpose(1, 0, 2).reshape(8, width).astype(F32)
    g1, b1, bq, bv, ab, g2, b2, pb = (params[i] for i in range(8))
    fc_b = small[:, 8:].reshape(chips, nc, per_ff)
    fc_b = lax.dynamic_index_in_dim(fc_b, core, 1, keepdims=False).reshape(ff_half).astype(F32)
    bq_half = lax.dynamic_slice_in_dim(bq, core * half, half)
    bv_half = lax.dynamic_slice_in_dim(bv, core * half, half)

    x_chip = grid.gather(layer_input[0], "c").reshape(nc * tok, width)
    dy_chip = grid.gather(cotangent[0], "c").reshape(nc * tok, width)

    def core_half(halves):
        first = core == 0
        keep = jnp.where(first, halves[0], halves[1])
        give = jnp.where(first, halves[1], halves[0])
        return pair(keep, grid.shift(give, "c", 1), core)

    q3 = w_qkv.reshape(per, 3, nc, half)
    wq = core_half([q3[:, :, i].reshape(per, 3 * half) for i in range(nc)])
    f3 = w_fc.reshape(per, chips, nc, per_ff)
    wb = core_half(
        [
            jnp.concatenate(
                [f3[:, :, i].reshape(per, ff_half), w_attn_out[:, i * half : (i + 1) * half]], -1
            )
            for i in range(nc)
        ]
    )
    wp = w_proj

    wq = grid.gather(wq, "z")
    wb, wq = lax.optimization_barrier((wb, wq))
    wq = grid.gather(wq, "y", axis=1)
    wb = grid.gather(wb, "z")
    wp, wb, wq = lax.optimization_barrier((wp, wb, wq))
    wq = grid.gather(wq, "d").reshape(width, 3 * half)
    wb = grid.gather(wb, "y", axis=1)

    x_float = x_chip.astype(F32)
    normed1, inv1, pre1 = norm_fwd(x_float, g1, b1)
    n1 = pre1.astype(BF)
    qkv = mm(n1, wq)
    queries = (qkv[:, :half] + bq_half).astype(BF)
    keys_loc = qkv[:, half : 2 * half].astype(BF)
    values_loc = (qkv[:, 2 * half :] + bv_half).astype(BF)
    keys_all = grid.gather(keys_loc, "z")
    values_loc, keys_all = lax.optimization_barrier((values_loc, keys_all))
    values_all = grid.gather(values_loc, "z")
    keys_all = grid.gather(keys_all, "y", axis=1).reshape(-1, half)
    values_all = grid.gather(values_all, "y", axis=1).reshape(-1, half)
    wb = grid.gather(wb, "d").reshape(width, ff_half + half)
    w_fc_half = wb[:, :ff_half]
    w_o = grid.gather(wb[:, ff_half:], "c", axis=1).reshape(width, width)
    wp = grid.gather(wp, "z")
    wp = grid.gather(wp, "y", axis=1)
    w_proj_half = grid.gather(wp, "d").reshape(ff_half, width)

    q_pos = chip_at * (nc * tok) + jnp.arange(nc * tok, dtype=jnp.int32)
    q_seg = lax.dynamic_slice_in_dim(seg_all, chip_at * (nc * tok), nc * tok)
    q_start = jnp.sum((seg_all[None, :] < q_seg[:, None]).astype(jnp.int32), 1)
    pos = jnp.stack([q_pos, q_start])
    length = keys_all.shape[0]
    blk = math.gcd(length, 256)
    last = chip_at * (nc * tok) + nc * tok
    bounds = jnp.stack([q_start[0] // blk, (last + blk - 1) // blk]).astype(jnp.int32)

    attn, lse = attn_fwd(bounds, queries, keys_all, values_all, pos)
    attn_full = grid.gather(attn, "c", axis=1).reshape(nc * tok, width)
    hid = x_float + mm(attn_full, w_o) + ab
    normed2, inv2, pre2 = norm_fwd(hid, g2, b2)
    n2 = pre2.astype(BF)
    pre_act = mm(n2, w_fc_half) + fc_b
    act_f, slope = gelu_pair(pre_act)
    act = act_f.astype(BF)

    dy_float = dy_chip.astype(F32)
    d_pre_f = mm(dy_chip, w_proj_half, NT) * slope
    d_pre = d_pre_f.astype(BF)
    d_n2_part = mm(d_pre, w_fc_half, NT)
    d_n2 = d_n2_part + grid.shift(d_n2_part, "c", 1)
    d_from2, g_ln2_gain, g_ln2_bias = norm_back(d_n2, normed2, inv2, g2)
    d_hid_f = dy_float + d_from2
    d_hid = d_hid_f.astype(BF)
    w_o_rows = lax.dynamic_slice_in_dim(w_o, core * half, half, 0)
    d_attn = mm(d_hid, w_o_rows, NT).astype(BF)

    def to_owner(grad, rows_per):
        grad = grad.reshape((nd, nz, ny) + rows_per + (grad.shape[-1],))
        grad = grid.scatter(grad, "d")
        grad = grid.scatter(grad, "y", axis=1)
        return grid.scatter(grad, "z")

    g_w_proj = to_owner(mm(act, dy_chip, TN), (per_ff,))
    g_w_fc = to_owner(mm(n2, d_pre, TN), (nc, per))

    def own_rows(value):
        return lax.dynamic_slice_in_dim(value, core * tok, tok, 0)

    def other_rows(value):
        return lax.dynamic_slice_in_dim(value, (1 - core) * tok, tok, 0)

    out_part = mm(act, w_proj_half)
    out = own_rows(hid + out_part) + grid.shift(other_rows(out_part), "c", 1) + pb
    out = out.astype(BF)

    d_q, d_k, d_v = attn_bwd(bounds, queries, keys_all, values_all, d_attn, attn, lse, pos)

    d_hid_cols = lax.dynamic_slice_in_dim(d_hid, core * half, half, 1)
    g_w_o = to_owner(mm(attn_full, d_hid_cols, TN), (nc, per))

    def to_position(value):
        value = value.reshape(nz, ny, nc * tok, half)
        return grid.scatter(grid.scatter(value, "y", axis=1), "z")

    d_keys = to_position(d_k)
    d_values = to_position(d_v)
    g_bias_query = jnp.sum(d_q, 0)
    g_bias_value = jnp.sum(d_values, 0)
    d_qkv = jnp.concatenate([d_q, d_keys, d_values], -1).astype(BF)
    g_w_qkv = to_owner(mm(n1, d_qkv, TN), (nc, per))
    d_n1_part = mm(d_qkv, wq, NT)
    d_n1 = own_rows(d_n1_part) + grid.shift(other_rows(d_n1_part), "c", 1)
    d_from1, g_ln1_gain, g_ln1_bias = norm_back(d_n1, own_rows(normed1), own_rows(inv1), g1)
    grad_in = (own_rows(d_hid_f) + d_from1).astype(BF)

    def both_halves(grad, parts):
        own = lax.dynamic_index_in_dim(grad, core, 0, keepdims=False)
        give = lax.dynamic_index_in_dim(grad, 1 - core, 0, keepdims=False)
        got = grid.shift(give, "c", 1)
        shape = (per, parts, grad.shape[-1] // parts)
        return pair(own.reshape(shape), got.reshape(shape), core, 2).reshape(per, -1)

    out_qkv = both_halves(g_w_qkv, 3)
    out_w_o = both_halves(g_w_o, 1)
    out_fc = both_halves(g_w_fc, chips)

    def at_half(value):
        zero = jnp.zeros((half,), F32)
        return jnp.where(
            core == 0, jnp.concatenate([value, zero]), jnp.concatenate([zero, value])
        )

    g_bias_proj = jnp.sum(dy_float, 0)
    g_bias_attn_out = jnp.sum(d_hid_f, 0)
    vecs = jnp.stack(
        [
            g_ln1_gain,
            g_ln1_bias,
            at_half(g_bias_query),
            at_half(g_bias_value),
            0.5 * g_bias_attn_out,
            0.5 * g_ln2_gain,
            0.5 * g_ln2_bias,
            0.5 * g_bias_proj,
        ]
    )
    vecs = vecs.reshape(8, devs, per).transpose(1, 0, 2)
    g_fc_b = jnp.sum(d_pre_f, 0).reshape(chips, 1, ff_rows, per)
    mine = (lax.broadcasted_iota(jnp.int32, (1, nc, 1, 1), 1) == core).astype(F32)
    g_fc_b = (g_fc_b * mine).reshape(devs, ff_rows, per)
    vecs = jnp.concatenate([vecs, g_fc_b], 1).reshape(nd, nz, ny, nc, 8 + ff_rows, per)
    vecs = grid.scatter(vecs, "d", wire=F32)
    vecs = grid.scatter(vecs, "z", wire=F32)
    vecs = grid.scatter(vecs, "y", wire=F32)
    vecs = grid.scatter(vecs, "c", wire=F32)

    return (
        out[None],
        grad_in[None],
        vecs[0],
        vecs[1],
        out_qkv,
        vecs[2],
        vecs[3],
        out_w_o,
        vecs[4],
        vecs[5],
        vecs[6],
        out_fc,
        vecs[8:].reshape(per_ff),
        g_w_proj,
        vecs[7],
    )


def solution(mesh):
    flat = P(("dp", "seq"))
    rows = P(("dp", "seq"), None)
    act = P("dp", "seq", None)
    return jax.shard_map(
        functools.partial(body, Grid(mesh)),
        mesh=mesh,
        in_specs=(
            act,
            flat,
            flat,
            rows,
            flat,
            flat,
            rows,
            flat,
            flat,
            flat,
            rows,
            flat,
            rows,
            flat,
            P("dp", "seq"),
            act,
        ),
        out_specs=(
            act,
            act,
            flat,
            flat,
            rows,
            flat,
            flat,
            rows,
            flat,
            flat,
            flat,
            rows,
            flat,
            rows,
            flat,
        ),
        check_vma=False,
    )
```
